128 devices in a mesh: freq: 16 (over x, y), slab: 8 (over z, core).
Axes of the slice: x: 4, y: 4, z: 4, core: 2. Of those that a mesh axis runs over, the one named last changes fastest.
Arguments:
- fine_model: bfloat16 [2048, 2048], P(('freq', 'slab')), may hold values from 0.5 to 2
- resample: bfloat16 [16, 1024, 2048], P('freq', 'slab'), may hold values from -0.125 to 0.125
- lateral: bfloat16 [2048, 2048], replicated, may hold values from -0.0625 to 0.0625
- shift: float32 [16], P('freq'), may hold values from 0.5 to 4
- source: float32 [16, 1024, 2048], P('freq', 'slab'), may hold values from -6 to 6
- receiver: float32 [16, 1024, 2048], P('freq', 'slab'), may hold values from -6 to 6
Outputs:
- image: float32 [2048, 2048], P(('freq', 'slab'))
The draws below stay inside these ranges and needn't reach their ends.
All inputs are finite; a program needn't handle non-finite values.
Results may differ from the reference program's by a relative error of at most 0.0029.
Values may be sent and summed in bfloat16 or wider, within the bound.
A program may use at most 128 MiB of HBM per device.

```python
import math
import jax
import jax.numpy as jnp
from jax import lax

NL = 2048
SWEEPS = 8
NGROUPS = 16
NZF = 2048
CZT = 1024


def levels(rng, shape, split, smallest, largest):
    loudness, own = 1.0, jax.random.fold_in(rng, 6)
    for axis_at, shards_of in split:
        heights = jnp.exp(jax.random.uniform(jax.random.fold_in(own, axis_at), (shards_of,), jnp.float32, smallest / len(split), largest / len(split)))
        loudness = loudness * jnp.repeat(heights, shape[axis_at] // shards_of).reshape([-1 if axis == axis_at else 1 for axis in range(len(shape))])
    return loudness


def noise(rng, extent, scale, most, cuts=(), dtype=jnp.bfloat16):
    entries = jax.random.normal(rng, extent, jnp.float32) * scale
    if len(cuts) > 0:
        entries = levels(rng, extent, cuts, -0.22, 0.18) * entries
    return jnp.clip(entries, min=-most, max=most).astype(dtype)


def setup_inputs(seed: int = 0) -> dict:
    splits = jax.random.split(jax.random.key(seed), 7)
    fine_model = jnp.clip(0.5 + 1.5 * jax.random.uniform(splits[0], (NZF, NL), jnp.float32) ** levels(splits[0], (NZF, NL), ((0, 128),), -0.2, 0.2), 0.5, 2.0).astype(jnp.bfloat16)
    resample = noise(splits[1], (NGROUPS, CZT, NZF), NZF ** -0.5, 0.125, ((0, 16), (1, 8)))
    lateral = noise(splits[2], (NL, NL), (4 * NL) ** -0.5, 0.0625)
    shift = jnp.clip(jnp.exp(math.log(4.0) - 2.0794415 * jax.random.uniform(splits[3], (NGROUPS,), jnp.float32) ** levels(splits[3], (NGROUPS,), ((0, 16),), -0.2, 0.2)), 0.5, 4.0)
    source = noise(splits[4], (NGROUPS, CZT, NL), 1.0, 6.0, ((0, 16), (1, 8)), jnp.float32)
    receiver = noise(splits[5], (NGROUPS, CZT, NL), 1.0, 6.0, ((0, 16), (1, 8)), jnp.float32)
    return dict(fine_model=fine_model, resample=resample, lateral=lateral, shift=shift, source=source, receiver=receiver)


def reference(fine_model, resample, lateral, shift, source, receiver):
    def group(total, items):
        oper, factor, src, rec = items
        coarse = jnp.dot(oper, fine_model, preferred_element_type=jnp.float32)
        diag = 4.0 + factor * coarse * coarse
        field = jnp.zeros(src.shape, jnp.float32)
        for sweep in range(SWEEPS):
            padded = jnp.pad(field, ((1, 1), (0, 0)))
            beside = padded[2:] + padded[:-2]
            side = jnp.dot(field.astype(jnp.bfloat16), lateral, preferred_element_type=jnp.float32)
            field = (src + 0.5 * beside + side) / diag
        partial_img = (field * rec).astype(jnp.bfloat16)
        term = lax.dot_general(oper, partial_img, (((0,), (0,)), ((), ())), preferred_element_type=jnp.float32)
        return total + term, None

    start = jnp.zeros(fine_model.shape, jnp.float32)
    image, unused = lax.scan(group, start, (resample, shift, source, receiver))
    return image
```

```python
import jax
import jax.numpy as jnp
from jax import lax
from jax.sharding import PartitionSpec as P

SWEEPS = 8
HALO = 8


def with_halo(value, size):
    up = [(i, i + 1) for i in range(size - 1)]
    down = [(i + 1, i) for i in range(size - 1)]
    before = lax.ppermute(value[-HALO:], "slab", up)
    after = lax.ppermute(value[:HALO], "slab", down)
    return jnp.concatenate([before, value, after], axis=0)


def shards(fine_model, resample, lateral, shift, source, receiver):
    freqs, slabs = lax.axis_size("freq"), lax.axis_size("slab")
    oper = resample[0]
    rows = oper.shape[0]
    every = lax.all_gather(oper, "slab", axis=0, tiled=True)
    wide = with_halo(oper, slabs)
    src = with_halo(source[0], slabs)
    model = lax.all_gather(fine_model, ("freq", "slab"), axis=0, tiled=True)
    coarse = jnp.dot(wide, model, preferred_element_type=jnp.float32)
    at = lax.axis_index("slab") * rows - HALO + lax.broadcasted_iota(jnp.int32, (rows + 2 * HALO, 1), 0)
    inside = (at >= 0) & (at < rows * slabs)
    inv = jnp.where(inside, 1.0 / (4.0 + shift[0] * coarse * coarse), 0.0)
    field = src * inv
    for sweep in range(1, SWEEPS):
        padded = jnp.pad(field, ((1, 1), (0, 0)))
        beside = padded[2:] + padded[:-2]
        side = jnp.dot(field.astype(jnp.bfloat16), lateral, preferred_element_type=jnp.float32)
        field = (src + 0.5 * beside + side) * inv
    part = (field[HALO:-HALO] * receiver[0]).astype(jnp.bfloat16)
    cols = lax.all_to_all(part, "slab", split_axis=1, concat_axis=0, tiled=True)
    term = lax.dot_general(every, cols, (((0,), (0,)), ((), ())), preferred_element_type=jnp.float32)
    mine = lax.psum_scatter(term, "freq", scatter_dimension=0, tiled=True)
    return lax.all_to_all(mine, "slab", split_axis=0, concat_axis=1, tiled=True)


def solution(mesh):
    in_specs = (
        P(("freq", "slab"), None),
        P("freq", "slab", None),
        P(),
        P("freq"),
        P("freq", "slab", None),
        P("freq", "slab", None),
    )
    out_specs = P(("freq", "slab"), None)
    return jax.shard_map(shards, mesh=mesh, in_specs=in_specs, out_specs=out_specs, check_vma=False)
```

```python
import functools

import jax
import jax.numpy as jnp
from jax import lax
from jax.experimental import pallas as pl
from jax.experimental.pallas import tpu as pltpu
from jax.sharding import PartitionSpec as P

SWEEPS = 8
HALO = 8
SIDE = 4
SLABS = 8
WIDE = 256
BLOCK = 128
F32, BF16 = jnp.float32, jnp.bfloat16


def with_halo(value, size):
    up = [(i, i + 1) for i in range(size - 1)]
    down = [(i + 1, i) for i in range(size - 1)]
    before = lax.ppermute(value[-HALO:], "slab", up)
    after = lax.ppermute(value[:HALO], "slab", down)
    return jnp.concatenate([before, value, after], axis=0)


def place():
    freq, slab = lax.axis_index("freq"), lax.axis_index("slab")
    return freq // SIDE, lax.rem(freq, SIDE), slab


def beyond(me, step, size):
    return lax.rem(me + step, size)


def send(src, dst, sems, index, to):
    copy = pltpu.make_async_remote_copy(
        src_ref=src, dst_ref=dst, send_sem=sems[0].at[index], recv_sem=sems[1].at[index],
        device_id=to, device_id_type=pl.DeviceIdType.MESH,
    )
    copy.start()
    return copy


def tail_kernel(part, every, image, turned, gathered, terms, sent, came, sums, came2, final,
                a2a_s, a2a_r, one_s, one_r, two_s, two_r, end_s, end_r):
    x, y, slab = place()
    freq = x * SIDE + y
    along_x = [{"freq": beyond(x, d, SIDE) * SIDE + y, "slab": slab} for d in range(1, SIDE)]
    along_y = [{"freq": x * SIDE + beyond(y, d, SIDE), "slab": slab} for d in range(1, SIDE)]
    line = [{"freq": freq, "slab": beyond(slab, d, SLABS)} for d in range(1, SLABS)]

    barrier = pltpu.get_barrier_semaphore()
    peers = along_x + along_y + line
    for peer in peers:
        pl.semaphore_signal(barrier, inc=1, device_id=peer, device_id_type=pl.DeviceIdType.MESH)
    for s in range(SLABS):
        turned[s] = part[:, s * WIDE:(s + 1) * WIDE].T
    pl.semaphore_wait(barrier, len(peers))

    lanes = pl.ds(pl.multiple_of(slab * BLOCK, BLOCK), BLOCK)
    copies = []
    for d in range(1, SLABS):
        copies.append(send(turned.at[beyond(slab, d, SLABS)], gathered.at[:, lanes], (a2a_s, a2a_r), d - 1, line[d - 1]))
    gathered[:, lanes] = turned[slab]
    for copy in copies:
        copy.wait()

    for n in range(SIDE):
        term = jnp.dot(gathered[...], every[:, n * 512:(n + 1) * 512], preferred_element_type=F32)
        terms[0, n] = term[:BLOCK]
        sent[0, n] = term[:BLOCK].astype(BF16)
        for m in range(SIDE):
            piece = term[BLOCK:, m * BLOCK:(m + 1) * BLOCK]
            terms[1, m, :, n * BLOCK:(n + 1) * BLOCK] = piece
            sent[1, m, :, n * BLOCK:(n + 1) * BLOCK] = piece.astype(BF16)

    first = []
    for half, (me, ways) in enumerate(((x, along_x), (y, along_y))):
        for d in range(1, SIDE):
            first.append(send(sent.at[half, beyond(me, d, SIDE)], came.at[half, d - 1],
                              (one_s, one_r), half * 3 + d - 1, ways[d - 1]))
    second = []
    for half, (me, other, ways) in enumerate(((x, y, along_y), (y, x, along_x))):
        for d in range(3):
            first[half * 3 + d].wait()
        total = terms[half, me]
        for d in range(3):
            total += came[half, d].astype(F32)
        for m in range(SIDE):
            sums[half, m] = total[:, m * BLOCK:(m + 1) * BLOCK]
        for d in range(1, SIDE):
            second.append(send(sums.at[half, beyond(other, d, SIDE)], came2.at[half, d - 1],
                               (two_s, two_r), half * 3 + d - 1, ways[d - 1]))
    for half, other in enumerate((y, x)):
        for d in range(3):
            second[half * 3 + d].wait()
        total = sums[half, other]
        for d in range(3):
            total += came2[half, d]
        flat = total.T
        for s in range(SLABS):
            final[s, :, half * BLOCK:(half + 1) * BLOCK] = flat[s * 16:(s + 1) * 16]
    here = pl.ds(pl.multiple_of(slab * WIDE, WIDE), WIDE)
    ends = []
    for d in range(1, SLABS):
        ends.append(send(final.at[beyond(slab, d, SLABS)], image.at[:, here], (end_s, end_r), d - 1, line[d - 1]))
    image[:, here] = final[slab]
    for copy in ends:
        copy.wait()


def tail(part, every):
    vmem = pl.BlockSpec(memory_space=pltpu.VMEM)
    dma = pltpu.SemaphoreType.DMA
    return pl.pallas_call(
        tail_kernel,
        name="tail",
        out_shape=jax.ShapeDtypeStruct((16, 2048), F32),
        in_specs=[vmem, vmem],
        out_specs=vmem,
        scratch_shapes=[
            pltpu.VMEM((SLABS, WIDE, BLOCK), BF16),
            pltpu.VMEM((WIDE, SLABS * BLOCK), BF16),
            pltpu.VMEM((2, SIDE, BLOCK, 512), F32),
            pltpu.VMEM((2, SIDE, BLOCK, 512), BF16),
            pltpu.VMEM((2, 3, BLOCK, 512), BF16),
            pltpu.VMEM((2, SIDE, BLOCK, BLOCK), F32),
            pltpu.VMEM((2, 3, BLOCK, BLOCK), F32),
            pltpu.VMEM((SLABS, 16, WIDE), F32),
            dma((7,)), dma((7,)), dma((6,)), dma((6,)), dma((6,)), dma((6,)), dma((7,)), dma((7,)),
        ],
        compiler_params=pltpu.CompilerParams(collective_id=0, has_side_effects=True, vmem_limit_bytes=40 << 20),
    )(part, every)


def shards(fine_model, resample, lateral, shift, source, receiver):
    slabs = lax.axis_size("slab")
    oper = resample[0]
    rows = oper.shape[0]
    every = lax.all_gather(oper, "slab", axis=0, tiled=True)
    wide = with_halo(oper, slabs)
    src = with_halo(source[0], slabs)
    model = lax.all_gather(fine_model, ("freq", "slab"), axis=0, tiled=True)
    coarse = jnp.dot(wide, model, preferred_element_type=F32)
    at = lax.axis_index("slab") * rows - HALO + lax.broadcasted_iota(jnp.int32, (rows + 2 * HALO, 1), 0)
    inside = (at >= 0) & (at < rows * slabs)
    inv = jnp.where(inside, 1.0 / (4.0 + shift[0] * coarse * coarse), 0.0)
    field = src * inv
    for sweep in range(1, SWEEPS):
        padded = jnp.pad(field, ((1, 1), (0, 0)))
        beside = padded[2:] + padded[:-2]
        side = jnp.dot(field.astype(BF16), lateral, preferred_element_type=F32)
        field = (src + 0.5 * beside + side) * inv
    part = (field[HALO:-HALO] * receiver[0]).astype(BF16)
    return tail(part, every)


def solution(mesh):
    in_specs = (
        P(("freq", "slab"), None),
        P("freq", "slab", None),
        P(),
        P("freq"),
        P("freq", "slab", None),
        P("freq", "slab", None),
    )
    out_specs = P(("freq", "slab"), None)
    return jax.shard_map(shards, mesh=mesh, in_specs=in_specs, out_specs=out_specs, check_vma=False)
```

```python
import functools

import jax
import jax.numpy as jnp
from jax import lax
from jax.experimental import pallas as pl
from jax.experimental.pallas import tpu as pltpu
from jax.sharding import PartitionSpec as P

SWEEPS = 8
HALO = 8
SIDE = 4
SLABS = 8
ROWS = 128
TALL = ROWS + 2 * HALO
CHIP = 2 * ROWS
NL = 2048
HALF = NL // 2
PATH = HALF // 2
WIDE = NL // SLABS
BLOCK = 128
F32, BF16 = jnp.float32, jnp.bfloat16
MESH = pl.DeviceIdType.MESH


def turn(value, size):
    return lax.rem(value, size)


def ds(start, size, multiple=128):
    return pl.ds(pl.multiple_of(start, multiple), size)


class Links:
    def __init__(self, send, recv):
        self.send, self.recv, self.used, self.all = send, recv, 0, []

    def start(self, src, dst, to):
        copy = pltpu.make_async_remote_copy(
            src_ref=src, dst_ref=dst, send_sem=self.send.at[self.used], recv_sem=self.recv.at[self.used],
            device_id=to, device_id_type=MESH,
        )
        copy.start()
        self.used += 1
        self.all.append(copy)
        return copy

    def finish(self):
        for copy in self.all:
            copy.wait_send()


def migrate(fine, oper, lateral, shift, source, receiver, image,
            fa, fb, lhs, edge, every, lat, src, rec, invc, inv, field, narrow,
            turned, gathered, terms, sent, came, sums, came2, final, send_sem, recv_sem, local_sem):
    freq, slab = lax.axis_index("freq"), lax.axis_index("slab")
    x, y, z, core = freq // SIDE, turn(freq, SIDE), slab // 2, turn(slab, 2)
    other = 1 - core

    def at(dx=0, dy=0, dz=0, dc=0):
        return {"freq": turn(x + dx, SIDE) * SIDE + turn(y + dy, SIDE),
                "slab": turn(z + dz, SIDE) * 2 + turn(core + dc, 2)}

    links = Links(send_sem, recv_sem)
    line = [{"freq": freq, "slab": turn(slab + d, SLABS)} for d in range(1, SLABS)]

    here = ds(slab * ROWS, ROWS)
    mine = ds(core * 16, 16, 16)
    local = {}
    for name, a, b in (
        ("fa", fine.at[:, ds(core * HALF, PATH)], fa.at[x, y, z, mine]),
        ("fb", fine.at[:, ds(core * HALF + PATH, PATH)], fb.at[x, y, z, mine]),
        ("lhs", oper, lhs.at[ds(core * ROWS, ROWS)]),
        ("every", oper, every.at[here]),
        ("src", source, src.at[HALO:HALO + ROWS]),
        ("lat", lateral, lat),
        ("rec", receiver, rec),
    ):
        local[name] = pltpu.make_async_copy(a, b, local_sem.at[len(local)])
        local[name].start()

    barrier = pltpu.get_barrier_semaphore()
    peers = line + [at(dx=d, dc=e) for d in (1, 2, 3) for e in (0, 1)] + [at(dy=d, dc=e) for d in (1, 2, 3) for e in (0, 1)]
    for peer in peers:
        pl.semaphore_signal(barrier, inc=1, device_id=peer, device_id_type=MESH)
    pl.semaphore_wait(barrier, len(peers))

    one = {0: [], 1: []}
    for d in range(SIDE):
        for e in range(2):
            if d or e:
                column = turn(core + e, 2) * HALF
                one[0].append(links.start(fine.at[:, ds(column, PATH)], fa.at[x, y, z, mine], at(dy=d, dc=e)))
                one[1].append(links.start(fine.at[:, ds(column + PATH, PATH)], fb.at[x, y, z, mine], at(dx=d, dc=e)))
    rows = links.start(oper, lhs.at[ds(core * ROWS, ROWS)], at(dc=1))
    early = []
    for e in range(2):
        to = {"freq": freq, "slab": turn(z + 3 - 2 * core, SIDE) * 2 + turn(core + e, 2)}
        early.append(links.start(oper.at[ds(core * (ROWS - 16), 16, 16)], edge.at[other], to))
    late = [
        links.start(source.at[ROWS - HALO:ROWS], src.at[0:HALO], line[0]),
        links.start(source.at[0:HALO], src.at[HALO + ROWS:TALL], line[SLABS - 2]),
    ]

    def chunk(path, step, k):
        if path == 0:
            return fa.at[turn(x + step, SIDE), :, turn(z + k, SIDE)]
        return fb.at[:, turn(y + step, SIDE), turn(z + k, SIDE)]

    def ahead(path, step):
        return at(dx=step) if path == 0 else at(dy=step)

    order = (0, 3, 1, 2)
    two, three, passed = {}, {}, {}

    def spread(path, k):
        part = chunk(path, 0, order[k])
        three[path, k] = (links.start(part, part, ahead(path, 1)), links.start(part, part, ahead(path, 3)))

    def forward(path, k):
        if k < 2:
            three[path, k][0].wait_recv()
            part = chunk(path, 3, order[k])
            passed[path, k] = links.start(part, part, ahead(path, 1))
        else:
            three[path, k][1].wait_recv()
            part = chunk(path, 1, order[k])
            passed[path, k] = links.start(part, part, ahead(path, 3))

    for path in (0, 1):
        local["fa" if path == 0 else "fb"].wait()
        for copy in one[path]:
            copy.wait_recv()
        part = chunk(path, 0, 0)
        for k in (1, 2, 3):
            two[path, k] = links.start(part, part, at(dz=SIDE - order[k]))
        spread(path, 0)
    for k in (1, 2):
        for path in (0, 1):
            two[path, k].wait_recv()
            spread(path, k)
    for path in (0, 1):
        forward(path, 0)
    for path in (0, 1):
        two[path, 3].wait_recv()
        spread(path, 3)

    local["every"].wait()
    whole = every.at[here]
    beside_core = links.start(whole, whole, at(dc=1))
    along = (links.start(whole, whole, at(dz=1)), links.start(whole, whole, at(dz=3)))

    for k in (1, 2, 3):
        for path in (0, 1):
            forward(path, k)

    for copy in early:
        copy.wait_recv()
    lhs[CHIP:CHIP + HALO] = edge[0, 16 - HALO:16]
    lhs[CHIP + HALO:CHIP + 2 * HALO] = edge[1, 0:HALO]
    local["lhs"].wait()
    rows.wait_recv()
    swapped = []
    for path, model in ((0, fa), (1, fb)):
        for k in range(SIDE):
            three[path, k][1 if k < 2 else 0].wait_recv()
            passed[path, k].wait_recv()
        columns = slice(path * PATH, (path + 1) * PATH)
        coarse = jnp.dot(lhs[...], model[...].reshape(NL, PATH), preferred_element_type=F32)
        part = 1.0 / (4.0 + shift[0] * coarse * coarse)
        invc[HALO:HALO + CHIP, columns] = part[:CHIP]
        invc[0:HALO, columns] = jnp.where(z > 0, part[CHIP:CHIP + HALO], 0.0)
        invc[HALO + CHIP:, columns] = jnp.where(z < SIDE - 1, part[CHIP + HALO:], 0.0)
        to = ds(core * HALF + path * PATH, PATH)
        swapped.append(links.start(invc.at[ds(other * ROWS, TALL), columns], inv.at[:, to], at(dc=1)))
        inv[:, to] = invc[ds(core * ROWS, TALL), columns]

    local["src"].wait()
    for copy in late + swapped:
        copy.wait_recv()
    for n in range(SIDE):
        columns = slice(n * 512, (n + 1) * 512)
        value = src[:, columns] * inv[:, columns]
        field[0, :, columns] = value
        narrow[0, :, columns] = value.astype(BF16)
    local["lat"].wait()
    local["rec"].wait()
    forwarded, crossed = [], []
    for sweep in range(1, SWEEPS):
        old, new = (sweep - 1) % 2, sweep % 2
        for n in range(SIDE):
            columns = slice(n * 512, (n + 1) * 512)
            side = jnp.dot(narrow[old], lat[:, columns], preferred_element_type=F32)
            before = field[old, :, columns]
            beside = pltpu.roll(before, 1, 0) + pltpu.roll(before, TALL - 1, 0)
            value = (src[:, columns] + 0.5 * beside + side) * inv[:, columns]
            if sweep < SWEEPS - 1:
                field[new, :, columns] = value
                narrow[new, :, columns] = value.astype(BF16)
            else:
                part = value[HALO:HALO + ROWS] * rec[:, columns]
                for m in range(2):
                    turned[2 * n + m] = part[:, m * WIDE:(m + 1) * WIDE].T.astype(BF16)
        if sweep == 2:
            along[0].wait_recv()
            block = turn(z + 3, SIDE) * 2 + core
            part = every.at[ds(block * ROWS, ROWS // 2, 64)]
            forwarded.append(links.start(part, part, at(dz=1)))
            part = every.at[ds(block * ROWS, ROWS)]
            crossed.append(links.start(part, part, at(dc=1)))
            along[1].wait_recv()
            block = turn(z + 1, SIDE) * 2 + core
            part = every.at[ds(block * ROWS + ROWS // 2, ROWS // 2, 64)]
            forwarded.append(links.start(part, part, at(dz=3)))
            part = every.at[ds(block * ROWS, ROWS)]
            crossed.append(links.start(part, part, at(dc=1)))
        if sweep == 6:
            for copy in forwarded:
                copy.wait_recv()
            block = turn(z + 2, SIDE) * 2 + core
            part = every.at[ds(block * ROWS, ROWS)]
            crossed.append(links.start(part, part, at(dc=1)))

    copies = []
    for d in range(1, SLABS):
        copies.append(links.start(turned.at[turn(slab + d, SLABS)], gathered.at[:, here], line[d - 1]))
    gathered[:, here] = turned[slab]
    beside_core.wait_recv()
    for copy in crossed + copies:
        copy.wait_recv()

    for n in range(SIDE):
        term = jnp.dot(gathered[...], every[:, n * 512:(n + 1) * 512], preferred_element_type=F32)
        terms[0, n] = term[:BLOCK]
        sent[0, n] = term[:BLOCK].astype(BF16)
        for m in range(SIDE):
            piece = term[BLOCK:, m * BLOCK:(m + 1) * BLOCK]
            terms[1, m, :, n * BLOCK:(n + 1) * BLOCK] = piece
            sent[1, m, :, n * BLOCK:(n + 1) * BLOCK] = piece.astype(BF16)
    first, second = {}, {}
    for half, me in ((0, x), (1, y)):
        for d in range(1, SIDE):
            first[half, d] = links.start(sent.at[half, turn(me + d, SIDE)], came.at[half, d - 1], ahead(half, d))
    for half, me, it in ((0, x, y), (1, y, x)):
        total = terms[half, me]
        for d in range(1, SIDE):
            first[half, d].wait_recv()
            total += came[half, d - 1].astype(F32)
        for m in range(SIDE):
            sums[half, m] = total[:, m * BLOCK:(m + 1) * BLOCK]
        for d in range(1, SIDE):
            second[half, d] = links.start(sums.at[half, turn(it + d, SIDE)], came2.at[half, d - 1], ahead(1 - half, d))
    for half, it in ((0, y), (1, x)):
        total = sums[half, it]
        for d in range(1, SIDE):
            second[half, d].wait_recv()
            total += came2[half, d - 1]
        flat = total.T
        for s in range(SLABS):
            final[s, :, half * BLOCK:(half + 1) * BLOCK] = flat[s * 16:(s + 1) * 16]
    to = ds(slab * WIDE, WIDE)
    ends = []
    for d in range(1, SLABS):
        ends.append(links.start(final.at[turn(slab + d, SLABS)], image.at[:, to], line[d - 1]))
    image[:, to] = final[slab]
    for copy in ends:
        copy.wait_recv()
    links.finish()


COPIES = 96


def shards(fine_model, resample, lateral, shift, source, receiver):
    anywhere = pl.BlockSpec(memory_space=pl.ANY)
    vmem, dma = pltpu.VMEM, pltpu.SemaphoreType.DMA
    return pl.pallas_call(
        migrate,
        name="migrate",
        out_shape=jax.ShapeDtypeStruct((16, NL), F32),
        in_specs=[anywhere, anywhere, anywhere, pl.BlockSpec(memory_space=pltpu.SMEM), anywhere, anywhere],
        out_specs=pl.BlockSpec(memory_space=pltpu.VMEM),
        scratch_shapes=[
            vmem((SIDE, SIDE, SIDE, 32, PATH), BF16),
            vmem((SIDE, SIDE, SIDE, 32, PATH), BF16),
            vmem((CHIP + 2 * HALO, NL), BF16),
            vmem((2, 16, NL), BF16),
            vmem((SLABS * ROWS, NL), BF16),
            vmem((NL, NL), BF16),
            vmem((TALL, NL), F32),
            vmem((ROWS, NL), F32),
            vmem((CHIP + 2 * HALO, HALF), F32),
            vmem((TALL, NL), F32),
            vmem((2, TALL, NL), F32),
            vmem((2, TALL, NL), BF16),
            vmem((SLABS, WIDE, BLOCK), BF16),
            vmem((WIDE, SLABS * BLOCK), BF16),
            vmem((2, SIDE, BLOCK, 512), F32),
            vmem((2, SIDE, BLOCK, 512), BF16),
            vmem((2, 3, BLOCK, 512), BF16),
            vmem((2, SIDE, BLOCK, BLOCK), F32),
            vmem((2, 3, BLOCK, BLOCK), F32),
            vmem((SLABS, 16, WIDE), F32),
            dma((COPIES,)), dma((COPIES,)), dma((7,)),
        ],
        compiler_params=pltpu.CompilerParams(collective_id=0, has_side_effects=True, vmem_limit_bytes=56 << 20),
    )(fine_model, resample[0], lateral, shift, source[0], receiver[0])


def solution(mesh):
    in_specs = (
        P(("freq", "slab"), None),
        P("freq", "slab", None),
        P(),
        P("freq"),
        P("freq", "slab", None),
        P("freq", "slab", None),
    )
    out_specs = P(("freq", "slab"), None)
    return jax.shard_map(shards, mesh=mesh, in_specs=in_specs, out_specs=out_specs, check_vma=False)
```

```python
import functools

import jax
import jax.numpy as jnp
from jax import lax
from jax.experimental import pallas as pl
from jax.experimental.pallas import tpu as pltpu
from jax.sharding import PartitionSpec as P

SWEEPS = 8
HALO = 8
SIDE = 4
SLABS = 8
ROWS = 128
TALL = ROWS + 2 * HALO
CHIP = 2 * ROWS
NL = 2048
HALF = NL // 2
PATHS = (((1, 2, 0), 0, 384), ((2, 0, 1), 384, 384), ((0, 1, 2), 768, 256))
WIDE = NL // SLABS
BLOCK = 128
F32, BF16 = jnp.float32, jnp.bfloat16
MESH = pl.DeviceIdType.MESH


def turn(value, size):
    return lax.rem(value, size)


def ds(start, size, multiple=128):
    return pl.ds(pl.multiple_of(start, multiple), size)


class Links:
    def __init__(self, send, recv):
        self.send, self.recv, self.used, self.all = send, recv, 0, []

    def start(self, src, dst, to):
        copy = pltpu.make_async_remote_copy(
            src_ref=src, dst_ref=dst, send_sem=self.send.at[self.used], recv_sem=self.recv.at[self.used],
            device_id=to, device_id_type=MESH,
        )
        copy.start()
        self.used += 1
        self.all.append(copy)
        return copy

    def finish(self):
        for copy in self.all:
            copy.wait_send()


def migrate(fine, oper, lateral, shift, source, receiver, image,
            fa, fb, fc, lhs, edge, every, lat, src, rec, partial, invc, inv, field, narrow,
            turned, gathered, own, sent, came, sums, came2, final, send_sem, recv_sem, local_sem):
    freq, slab = lax.axis_index("freq"), lax.axis_index("slab")
    x, y, z, core = freq // SIDE, turn(freq, SIDE), slab // 2, turn(slab, 2)
    other = 1 - core

    def at(dx=0, dy=0, dz=0, dc=0):
        return {"freq": turn(x + dx, SIDE) * SIDE + turn(y + dy, SIDE),
                "slab": turn(z + dz, SIDE) * 2 + turn(core + dc, 2)}

    links = Links(send_sem, recv_sem)
    line = [{"freq": freq, "slab": turn(slab + d, SLABS)} for d in range(1, SLABS)]

    here = ds(slab * ROWS, ROWS)
    mine = ds(core * 16, 16, 16)
    local = {}
    for name, a, b in (
        (0, fine.at[:, ds(core * HALF, 384)], fa.at[x, y, z, mine]),
        (1, fine.at[:, ds(core * HALF + 384, 384)], fb.at[x, y, z, mine]),
        (2, fine.at[:, ds(core * HALF + 768, 256)], fc.at[x, y, z, mine]),
        ("lhs", oper, lhs.at[ds(core * ROWS, ROWS)]),
        ("every", oper, every.at[here]),
        ("src", source, src.at[HALO:HALO + ROWS]),
        ("lat", lateral, lat),
        ("rec", receiver, rec),
    ):
        local[name] = pltpu.make_async_copy(a, b, local_sem.at[len(local)])
        local[name].start()

    barrier = pltpu.get_barrier_semaphore()
    peers = line + [at(dx=d, dc=e) for d in (1, 2, 3) for e in (0, 1)] + [at(dy=d, dc=e) for d in (1, 2, 3) for e in (0, 1)]
    for peer in peers:
        pl.semaphore_signal(barrier, inc=1, device_id=peer, device_id_type=MESH)
    pl.semaphore_wait(barrier, len(peers))

    models = (fa, fb, fc)

    def along(axis, step, dc=0):
        return at(**{("dx", "dy", "dz")[axis]: step, "dc": dc})

    one, two, three, passed = {}, {}, {}, {}
    for path, (axes, first, size) in enumerate(PATHS):
        one[path] = [
            links.start(fine.at[:, ds(turn(core + e, 2) * HALF + first, size)], models[path].at[x, y, z, mine],
                        along(axes[0], d, e))
            for d in range(SIDE) for e in range(2) if d or e
        ]
    lined = []

    def part_of(block, quarter, quarters=1):
        return every.at[ds(block * ROWS + quarter * 32, 32 * quarters, 32)]

    def lend():
        part = part_of(slab, len(lined))
        lined.append((links.start(part, part, at(dz=1)), links.start(part, part, at(dz=3))))

    local["every"].wait()
    lend()
    order = (0, 3, 1, 2)

    def chunk(path, step, k, of_first=slice(None)):
        where = [x, y, z]
        axes = PATHS[path][0]
        where[axes[0]] = of_first
        where[axes[1]] = turn(where[axes[1]] + order[k], SIDE)
        where[axes[2]] = turn(where[axes[2]] + step, SIDE)
        return models[path].at[tuple(where)]

    def spread(path, k):
        part, axis = chunk(path, 0, k), PATHS[path][0][2]
        three[path, k] = (links.start(part, part, along(axis, 1)), links.start(part, part, along(axis, 3)))

    def forward(path, k):
        axis = PATHS[path][0][2]
        passed[path, k] = []
        for side, (came_from, to, of_first) in enumerate(((3, 1, slice(0, 2)), (1, 3, slice(2, 4)))):
            three[path, k][side].wait_recv()
            part = chunk(path, came_from, k, of_first)
            passed[path, k].append(links.start(part, part, along(axis, to)))

    every_path = range(len(PATHS))
    for path in every_path:
        local[path].wait()
        for copy in one[path]:
            copy.wait_recv()
        part, axis = chunk(path, 0, 0), PATHS[path][0][1]
        for k in (1, 2, 3):
            two[path, k] = links.start(part, part, along(axis, SIDE - order[k]))
            if k == 2:
                spread(path, 0)
    rows = links.start(oper, lhs.at[ds(core * ROWS, ROWS)], at(dc=1))
    early = []
    for e in range(2):
        to = {"freq": freq, "slab": turn(z + 3 - 2 * core, SIDE) * 2 + turn(core + e, 2)}
        early.append(links.start(oper.at[ds(core * (ROWS - 16), 16, 16)], edge.at[other], to))
    late = [
        links.start(source.at[ROWS - HALO:ROWS], src.at[0:HALO], line[0]),
        links.start(source.at[0:HALO], src.at[HALO + ROWS:TALL], line[SLABS - 2]),
    ]
    beside_core = links.start(every.at[here], every.at[here], at(dc=1))
    for k in (1, 2):
        for path in every_path:
            two[path, k].wait_recv()
            spread(path, k)
    for path in every_path:
        forward(path, 0)
    for path in every_path:
        two[path, 3].wait_recv()
        spread(path, 3)
    lend()
    for k in (1, 2, 3):
        for path in every_path:
            forward(path, k)
    lend()
    lend()

    for copy in early:
        copy.wait_recv()
    lhs[CHIP:CHIP + HALO] = edge[0, 16 - HALO:16]
    lhs[CHIP + HALO:CHIP + 2 * HALO] = edge[1, 0:HALO]
    local["lhs"].wait()
    rows.wait_recv()
    swapped = []

    def finish_coarse(path, coarse):
        axes, start, size = PATHS[path]
        columns = slice(start, start + size)
        part = 1.0 / (4.0 + shift[0] * coarse * coarse)
        invc[HALO:HALO + CHIP, columns] = part[:CHIP]
        invc[0:HALO, columns] = jnp.where(z > 0, part[CHIP:CHIP + HALO], 0.0)
        invc[HALO + CHIP:, columns] = jnp.where(z < SIDE - 1, part[CHIP + HALO:], 0.0)
        to = ds(core * HALF + start, size)
        swapped.append(links.start(invc.at[ds(other * ROWS, TALL), columns], inv.at[:, to], at(dc=1)))
        inv[:, to] = invc[ds(core * ROWS, TALL), columns]

    lefts, rights = {}, {}
    for k in range(SIDE):
        to = turn(x + (0, 3, 1, 2)[k], SIDE)
        lefts[0, k] = lefts[1, k] = lambda to=to: lhs[:, ds(to * 512, 512)]
        rights[0, k] = lambda to=to: fa[to].reshape(512, PATHS[0][2])
        rights[1, k] = lambda to=to: fb[to].reshape(512, PATHS[1][2])
        to = turn(y + (0, 3, 1, 2)[k], SIDE)
        lefts[2, k] = lambda to=to: jnp.concatenate([lhs[:, ds(m * 512 + to * BLOCK, BLOCK)] for m in range(SIDE)], axis=1)
        rights[2, k] = lambda to=to: fc[:, to].reshape(512, PATHS[2][2])

    for k in range(SIDE):
        for path, (axes, start, size) in enumerate(PATHS):
            if k == 3:
                if path == 0:
                    for step in range(SIDE):
                        for copy in passed[path, step]:
                            copy.wait_recv()
                else:
                    for copy in passed[path, k]:
                        copy.wait_recv()
            elif path:
                for copy in passed[path, k]:
                    copy.wait_recv()
            columns = slice(start, start + size)
            term = jnp.dot(lefts[path, k](), rights[path, k](), preferred_element_type=F32)
            if k == 0:
                partial[:, columns] = term
            elif k < 3:
                partial[:, columns] += term
            else:
                finish_coarse(path, partial[:, columns] + term)
    local["src"].wait()
    for copy in late + swapped:
        copy.wait_recv()
    for n in range(SIDE):
        columns = slice(n * 512, (n + 1) * 512)
        value = src[:, columns] * inv[:, columns]
        field[0, :, columns] = value
        narrow[0, :, columns] = value.astype(BF16)
    local["lat"].wait()
    local["rec"].wait()
    forwarded, crossed = [], []

    def pass_on(side, step, quarters):
        for quarter in range(SIDE):
            if quarter in quarters:
                lined[quarter][side].wait_recv()
                part = part_of(turn(z + 4 - step, SIDE) * 2 + core, quarter)
                forwarded.append(links.start(part, part, at(dz=step)))

    def cross(step):
        part = part_of(turn(z + step, SIDE) * 2 + core, 0, SIDE)
        crossed.append(links.start(part, part, at(dc=1)))

    pass_on(0, 1, (0, 1))
    for sweep in range(1, SWEEPS - 1):
        old, new = (sweep - 1) % 2, sweep % 2
        for n in range(SIDE):
            columns = slice(n * 512, (n + 1) * 512)
            side = jnp.dot(narrow[old], lat[:, columns], preferred_element_type=F32)
            before = field[old, :, columns]
            beside = pltpu.roll(before, 1, 0) + pltpu.roll(before, TALL - 1, 0)
            value = (src[:, columns] + 0.5 * beside + side) * inv[:, columns]
            field[new, :, columns] = value
            narrow[new, :, columns] = value.astype(BF16)
        if sweep == 1:
            pass_on(1, 3, (2, 3))
        if sweep == 2:
            for quarter in range(SIDE):
                if quarter < 2:
                    lined[quarter][1].wait_recv()
                else:
                    lined[quarter][0].wait_recv()
            cross(3)
            cross(1)
        if sweep == 5:
            for copy in forwarded:
                copy.wait_recv()
            cross(2)

    old = (SWEEPS - 2) % 2
    spans = {}
    for half in range(2):
        for pair in ((1, 2), (3, 4), (5, 6), (7, 0)):
            slices = [ds(turn(slab + d, SLABS) * WIDE + half * BLOCK, BLOCK) for d in pair]
            panel = jnp.concatenate([lat[:, columns] for columns in slices], axis=1)
            both = jnp.dot(narrow[old], panel, preferred_element_type=F32)
            for m, (d, columns) in enumerate(zip(pair, slices)):
                side = both[:, m * BLOCK:(m + 1) * BLOCK]
                before = field[old, :, columns]
                beside = pltpu.roll(before, 1, 0) + pltpu.roll(before, TALL - 1, 0)
                value = (src[:, columns] + 0.5 * beside + side) * inv[:, columns]
                part = (value[HALO:HALO + ROWS] * rec[:, columns]).T.astype(BF16)
                if d:
                    turned[half, d - 1] = part
                    spans[half, d] = links.start(turned.at[half, d - 1], gathered.at[half, :, here], line[d - 1])
                else:
                    gathered[half, :, here] = part

    beside_core.wait_recv()
    for copy in crossed:
        copy.wait_recv()
    first, second = {}, {}
    for half, me in ((0, x), (1, y)):
        for d in range(1, SLABS):
            spans[half, d].wait_recv()
        for d in (2, 1, 3, 0):
            to = turn(me + d, SIDE)
            if half == 0:
                panel = every[:, ds(to * 512, 512)]
            else:
                panel = jnp.concatenate([every[:, ds(m * 512 + to * BLOCK, BLOCK)] for m in range(SIDE)], axis=1)
            term = jnp.dot(gathered[half], panel, preferred_element_type=F32)
            if d:
                sent[half, d - 1] = term.astype(BF16)
                first[half, d] = links.start(sent.at[half, d - 1], came.at[half, d - 1], along(half, d))
            else:
                own[half] = term
    for half, it in ((0, y), (1, x)):
        total = own[half]
        for d in range(1, SIDE):
            first[half, d].wait_recv()
            total += came[half, d - 1].astype(F32)
        own[half] = total
        for m in range(SIDE):
            sums[half, m] = total[:, m * BLOCK:(m + 1) * BLOCK].astype(sums.dtype)
        for d in range(1, SIDE):
            second[half, d] = links.start(sums.at[half, turn(it + d, SIDE)], came2.at[half, d - 1], along(1 - half, d))
    for half, it in ((0, y), (1, x)):
        total = own[half, :, ds(it * BLOCK, BLOCK)]
        for d in range(1, SIDE):
            second[half, d].wait_recv()
            total += came2[half, d - 1].astype(F32)
        flat = total.T
        for s in range(SLABS):
            final[s, :, half * BLOCK:(half + 1) * BLOCK] = flat[s * 16:(s + 1) * 16]
    to = ds(slab * WIDE, WIDE)
    ends = []
    for d in range(1, SLABS):
        ends.append(links.start(final.at[turn(slab + d, SLABS)], image.at[:, to], line[d - 1]))
    image[:, to] = final[slab]
    for copy in ends:
        copy.wait_recv()
    links.finish()


COPIES = 160


def shards(fine_model, resample, lateral, shift, source, receiver):
    anywhere = pl.BlockSpec(memory_space=pl.ANY)
    vmem, dma = pltpu.VMEM, pltpu.SemaphoreType.DMA
    return pl.pallas_call(
        migrate,
        name="migrate",
        out_shape=jax.ShapeDtypeStruct((16, NL), F32),
        in_specs=[anywhere, anywhere, anywhere, pl.BlockSpec(memory_space=pltpu.SMEM), anywhere, anywhere],
        out_specs=pl.BlockSpec(memory_space=pltpu.VMEM),
        scratch_shapes=[
            *(vmem((SIDE, SIDE, SIDE, 32, size), BF16) for _, _, size in PATHS),
            vmem((CHIP + 2 * HALO, NL), BF16),
            vmem((2, 16, NL), BF16),
            vmem((SLABS * ROWS, NL), BF16),
            vmem((NL, NL), BF16),
            vmem((TALL, NL), F32),
            vmem((ROWS, NL), F32),
            vmem((CHIP + 2 * HALO, HALF), F32),
            vmem((CHIP + 2 * HALO, HALF), F32),
            vmem((TALL, NL), F32),
            vmem((2, TALL, NL), F32),
            vmem((2, TALL, NL), BF16),
            vmem((2, SLABS - 1, BLOCK, BLOCK), BF16),
            vmem((2, BLOCK, SLABS * BLOCK), BF16),
            vmem((2, BLOCK, 512), F32),
            vmem((2, 3, BLOCK, 512), BF16),
            vmem((2, 3, BLOCK, 512), BF16),
            vmem((2, SIDE, BLOCK, BLOCK), BF16),
            vmem((2, 3, BLOCK, BLOCK), BF16),
            vmem((SLABS, 16, WIDE), F32),
            dma((COPIES,)), dma((COPIES,)), dma((8,)),
        ],
        compiler_params=pltpu.CompilerParams(collective_id=0, has_side_effects=True, vmem_limit_bytes=56203264),
    )(fine_model, resample[0], lateral, shift, source[0], receiver[0])


def solution(mesh):
    in_specs = (
        P(("freq", "slab"), None),
        P("freq", "slab", None),
        P(),
        P("freq"),
        P("freq", "slab", None),
        P("freq", "slab", None),
    )
    out_specs = P(("freq", "slab"), None)
    return jax.shard_map(shards, mesh=mesh, in_specs=in_specs, out_specs=out_specs, check_vma=False)
```

```python
import functools

import jax
import jax.numpy as jnp
from jax import lax
from jax.experimental import pallas as pl
from jax.experimental.pallas import tpu as pltpu
from jax.sharding import PartitionSpec as P

SWEEPS = 8
HALO = 8
SIDE = 4
SLABS = 8
ROWS = 128
TALL = ROWS + 2 * HALO
CHIP = 2 * ROWS
NL = 2048
HALF = NL // 2
PATHS = (((1, 2, 0), 0, 384), ((2, 0, 1), 384, 384), ((0, 1, 2), 768, 256))
WIDE = NL // SLABS
BLOCK = 128
F32, BF16 = jnp.float32, jnp.bfloat16
MESH = pl.DeviceIdType.MESH


def turn(value, size):
    return lax.rem(value, size)


def ds(start, size, multiple=128):
    return pl.ds(pl.multiple_of(start, multiple), size)


class Links:
    def __init__(self, send, recv):
        self.send, self.recv, self.used, self.all = send, recv, 0, []

    def start(self, src, dst, to):
        copy = pltpu.make_async_remote_copy(
            src_ref=src, dst_ref=dst, send_sem=self.send.at[self.used], recv_sem=self.recv.at[self.used],
            device_id=to, device_id_type=MESH,
        )
        copy.start()
        self.used += 1
        self.all.append(copy)
        return copy

    def finish(self):
        for copy in self.all:
            copy.wait_send()


def migrate(fine, oper, lateral, shift, source, receiver, image,
            fa, fb, fc, lhs, edge, every, lat, src, rec, partial, invc, inv, field, narrow,
            turned, gathered, own, sent, came, sums, landed, send_sem, recv_sem, local_sem):
    freq, slab = lax.axis_index("freq"), lax.axis_index("slab")
    x, y, z, core = freq // SIDE, turn(freq, SIDE), slab // 2, turn(slab, 2)
    other = 1 - core

    def at(dx=0, dy=0, dz=0, dc=0):
        return {"freq": turn(x + dx, SIDE) * SIDE + turn(y + dy, SIDE),
                "slab": turn(z + dz, SIDE) * 2 + turn(core + dc, 2)}

    links = Links(send_sem, recv_sem)
    line = [{"freq": freq, "slab": turn(slab + d, SLABS)} for d in range(1, SLABS)]

    here = ds(slab * ROWS, ROWS)
    mine = ds(core * 16, 16, 16)
    local = {}
    for name, a, b in (
        (0, fine.at[:, ds(core * HALF, 384)], fa.at[x, y, z, mine]),
        (1, fine.at[:, ds(core * HALF + 384, 384)], fb.at[x, y, z, mine]),
        (2, fine.at[:, ds(core * HALF + 768, 256)], fc.at[x, y, z, mine]),
        ("lhs", oper, lhs.at[ds(core * ROWS, ROWS)]),
        ("every", oper, every.at[here]),
        ("src", source, src.at[HALO:HALO + ROWS]),
        ("lat", lateral, lat),
        ("rec", receiver, rec),
    ):
        local[name] = pltpu.make_async_copy(a, b, local_sem.at[len(local)])
        local[name].start()

    barrier = pltpu.get_barrier_semaphore()
    peers = line + [at(dx=d, dc=e) for d in (1, 2, 3) for e in (0, 1)] + [at(dy=d, dc=e) for d in (1, 2, 3) for e in (0, 1)]
    for peer in peers:
        pl.semaphore_signal(barrier, inc=1, device_id=peer, device_id_type=MESH)
    pl.semaphore_wait(barrier, len(peers))

    models = (fa, fb, fc)

    def along(axis, step, dc=0):
        return at(**{("dx", "dy", "dz")[axis]: step, "dc": dc})

    one, two, three, passed = {}, {}, {}, {}
    for path, (axes, first, size) in enumerate(PATHS):
        one[path] = [
            links.start(fine.at[:, ds(turn(core + e, 2) * HALF + first, size)], models[path].at[x, y, z, mine],
                        along(axes[0], d, e))
            for d in range(SIDE) for e in range(2) if d or e
        ]
    lined = []

    def part_of(block, quarter, quarters=1):
        return every.at[ds(block * ROWS + quarter * 32, 32 * quarters, 32)]

    def lend():
        part = part_of(slab, len(lined))
        lined.append((links.start(part, part, at(dz=1)), links.start(part, part, at(dz=3))))

    local["every"].wait()
    lend()
    order = (0, 3, 1, 2)

    def chunk(path, step, k, of_first=slice(None)):
        where = [x, y, z]
        axes = PATHS[path][0]
        where[axes[0]] = of_first
        where[axes[1]] = turn(where[axes[1]] + order[k], SIDE)
        where[axes[2]] = turn(where[axes[2]] + step, SIDE)
        return models[path].at[tuple(where)]

    def spread(path, k):
        part, axis = chunk(path, 0, k), PATHS[path][0][2]
        three[path, k] = (links.start(part, part, along(axis, 1)), links.start(part, part, along(axis, 3)))

    def forward(path, k):
        axis = PATHS[path][0][2]
        passed[path, k] = []
        for side, (came_from, to, of_first) in enumerate(((3, 1, slice(0, 2)), (1, 3, slice(2, 4)))):
            three[path, k][side].wait_recv()
            part = chunk(path, came_from, k, of_first)
            passed[path, k].append(links.start(part, part, along(axis, to)))

    every_path = range(len(PATHS))
    for path in every_path:
        local[path].wait()
        for copy in one[path]:
            copy.wait_recv()
        part, axis = chunk(path, 0, 0), PATHS[path][0][1]
        for k in (1, 2, 3):
            two[path, k] = links.start(part, part, along(axis, SIDE - order[k]))
            if k == 2:
                spread(path, 0)
    rows = links.start(oper, lhs.at[ds(core * ROWS, ROWS)], at(dc=1))
    early = []
    for e in range(2):
        to = {"freq": freq, "slab": turn(z + 3 - 2 * core, SIDE) * 2 + turn(core + e, 2)}
        early.append(links.start(oper.at[ds(core * (ROWS - 16), 16, 16)], edge.at[other], to))
    late = [
        links.start(source.at[ROWS - HALO:ROWS], src.at[0:HALO], line[0]),
        links.start(source.at[0:HALO], src.at[HALO + ROWS:TALL], line[SLABS - 2]),
    ]
    beside_core = links.start(every.at[here], every.at[here], at(dc=1))
    for k in (1, 2):
        for path in every_path:
            two[path, k].wait_recv()
            spread(path, k)
    for path in every_path:
        forward(path, 0)
    for path in every_path:
        two[path, 3].wait_recv()
        spread(path, 3)
    lend()
    for k in (1, 2, 3):
        for path in every_path:
            forward(path, k)
    lend()
    lend()

    for copy in early:
        copy.wait_recv()
    lhs[CHIP:CHIP + HALO] = edge[0, 16 - HALO:16]
    lhs[CHIP + HALO:CHIP + 2 * HALO] = edge[1, 0:HALO]
    local["lhs"].wait()
    rows.wait_recv()
    swapped = []

    def finish_coarse(path, coarse):
        axes, start, size = PATHS[path]
        columns = slice(start, start + size)
        part = 1.0 / (4.0 + shift[0] * coarse * coarse)
        invc[HALO:HALO + CHIP, columns] = part[:CHIP]
        invc[0:HALO, columns] = jnp.where(z > 0, part[CHIP:CHIP + HALO], 0.0)
        invc[HALO + CHIP:, columns] = jnp.where(z < SIDE - 1, part[CHIP + HALO:], 0.0)
        to = ds(core * HALF + start, size)
        swapped.append(links.start(invc.at[ds(other * ROWS, TALL), columns], inv.at[:, to], at(dc=1)))
        inv[:, to] = invc[ds(core * ROWS, TALL), columns]

    lefts, rights = {}, {}
    for k in range(SIDE):
        to = turn(x + (0, 3, 1, 2)[k], SIDE)
        lefts[0, k] = lefts[1, k] = lambda to=to: lhs[:, ds(to * 512, 512)]
        rights[0, k] = lambda to=to: fa[to].reshape(512, PATHS[0][2])
        rights[1, k] = lambda to=to: fb[to].reshape(512, PATHS[1][2])
        to = turn(y + (0, 3, 1, 2)[k], SIDE)
        lefts[2, k] = lambda to=to: jnp.concatenate([lhs[:, ds(m * 512 + to * BLOCK, BLOCK)] for m in range(SIDE)], axis=1)
        rights[2, k] = lambda to=to: fc[:, to].reshape(512, PATHS[2][2])

    for k in range(SIDE):
        for path, (axes, start, size) in enumerate(PATHS):
            if k == 3:
                if path == 0:
                    for step in range(SIDE):
                        for copy in passed[path, step]:
                            copy.wait_recv()
                else:
                    for copy in passed[path, k]:
                        copy.wait_recv()
            elif path:
                for copy in passed[path, k]:
                    copy.wait_recv()
            columns = slice(start, start + size)
            term = jnp.dot(lefts[path, k](), rights[path, k](), preferred_element_type=F32)
            if k == 0:
                partial[:, columns] = term
            elif k < 3:
                partial[:, columns] += term
            else:
                finish_coarse(path, partial[:, columns] + term)
    local["src"].wait()
    for copy in late + swapped:
        copy.wait_recv()
    for n in range(SIDE):
        columns = slice(n * 512, (n + 1) * 512)
        value = src[:, columns] * inv[:, columns]
        field[0, :, columns] = value
        narrow[0, :, columns] = value.astype(BF16)
    local["lat"].wait()
    local["rec"].wait()
    forwarded, crossed = [], []

    def pass_on(side, step, quarters):
        for quarter in range(SIDE):
            if quarter in quarters:
                lined[quarter][side].wait_recv()
                part = part_of(turn(z + 4 - step, SIDE) * 2 + core, quarter)
                forwarded.append(links.start(part, part, at(dz=step)))

    def cross(step):
        part = part_of(turn(z + step, SIDE) * 2 + core, 0, SIDE)
        crossed.append(links.start(part, part, at(dc=1)))

    pass_on(0, 1, (0, 1))
    for sweep in range(1, SWEEPS - 1):
        old, new = (sweep - 1) % 2, sweep % 2
        for n in range(SIDE):
            columns = slice(n * 512, (n + 1) * 512)
            side = jnp.dot(narrow[old], lat[:, columns], preferred_element_type=F32)
            before = field[old, :, columns]
            beside = pltpu.roll(before, 1, 0) + pltpu.roll(before, TALL - 1, 0)
            value = (src[:, columns] + 0.5 * beside + side) * inv[:, columns]
            field[new, :, columns] = value
            narrow[new, :, columns] = value.astype(BF16)
        if sweep == 1:
            pass_on(1, 3, (2, 3))
        if sweep == 2:
            for quarter in range(SIDE):
                if quarter < 2:
                    lined[quarter][1].wait_recv()
                else:
                    lined[quarter][0].wait_recv()
            cross(3)
            cross(1)
        if sweep == 5:
            for copy in forwarded:
                copy.wait_recv()
            cross(2)

    old = (SWEEPS - 2) % 2
    spans = {}
    for half in range(2):
        for pair in ((1, 2), (3, 4), (5, 6), (7, 0)):
            slices = [ds(turn(slab + d, SLABS) * WIDE + half * BLOCK, BLOCK) for d in pair]
            panel = jnp.concatenate([lat[:, columns] for columns in slices], axis=1)
            both = jnp.dot(narrow[old], panel, preferred_element_type=F32)
            for m, (d, columns) in enumerate(zip(pair, slices)):
                side = both[:, m * BLOCK:(m + 1) * BLOCK]
                before = field[old, :, columns]
                beside = pltpu.roll(before, 1, 0) + pltpu.roll(before, TALL - 1, 0)
                value = (src[:, columns] + 0.5 * beside + side) * inv[:, columns]
                part = (value[HALO:HALO + ROWS] * rec[:, columns]).T.astype(BF16)
                if d:
                    turned[half, d - 1] = part
                    spans[half, d] = links.start(turned.at[half, d - 1], gathered.at[half, :, here], line[d - 1])
                else:
                    gathered[half, :, here] = part

    beside_core.wait_recv()
    for copy in crossed:
        copy.wait_recv()
    first, second = {}, []
    for half, me in ((0, x), (1, y)):
        for d in range(1, SLABS):
            spans[half, d].wait_recv()
        for d in (2, 1, 3, 0):
            to = turn(me + d, SIDE)
            if half == 0:
                panel = every[:, ds(to * 512, 512)]
            else:
                panel = jnp.concatenate([every[:, ds(m * 512 + to * BLOCK, BLOCK)] for m in range(SIDE)], axis=1)
            term = jnp.dot(gathered[half], panel, preferred_element_type=F32)
            if d:
                sent[half, d - 1] = term.astype(BF16)
                first[half, d] = links.start(sent.at[half, d - 1], came.at[half, d - 1], along(half, d))
            else:
                own[half] = term
    for half, it in ((0, y), (1, x)):
        total = own[half]
        for d in range(1, SIDE):
            first[half, d].wait_recv()
            total += came[half, d - 1].astype(F32)
        flat = total.T.astype(sums.dtype)
        for m in range(SIDE):
            for n in range(SLABS):
                sums[half, m, n] = flat[m * BLOCK + n * 16:m * BLOCK + (n + 1) * 16]
        to = ds(slab * WIDE + half * BLOCK, BLOCK)
        for d in (2, 1, 3, 0):
            for e in (4, 3, 5, 2, 6, 1, 7, 0):
                if d or e:
                    peer = along(1 - half, d)
                    peer["slab"] = turn(slab + e, SLABS)
                    second.append(links.start(sums.at[half, turn(it + d, SIDE), peer["slab"]], landed.at[d, :, to], peer))
        landed[0, :, to] = sums[half, it, slab]
    for copy in second:
        copy.wait_recv()
    image[...] = ((landed[0].astype(F32) + landed[1].astype(F32)) + (landed[2].astype(F32) + landed[3].astype(F32)))
    links.finish()


COPIES = 210


def shards(fine_model, resample, lateral, shift, source, receiver):
    anywhere = pl.BlockSpec(memory_space=pl.ANY)
    vmem, dma = pltpu.VMEM, pltpu.SemaphoreType.DMA
    return pl.pallas_call(
        migrate,
        name="migrate",
        out_shape=jax.ShapeDtypeStruct((16, NL), F32),
        in_specs=[anywhere, anywhere, anywhere, pl.BlockSpec(memory_space=pltpu.SMEM), anywhere, anywhere],
        out_specs=pl.BlockSpec(memory_space=pltpu.VMEM),
        scratch_shapes=[
            *(vmem((SIDE, SIDE, SIDE, 32, size), BF16) for _, _, size in PATHS),
            vmem((CHIP + 2 * HALO, NL), BF16),
            vmem((2, 16, NL), BF16),
            vmem((SLABS * ROWS, NL), BF16),
            vmem((NL, NL), BF16),
            vmem((TALL, NL), F32),
            vmem((ROWS, NL), F32),
            vmem((CHIP + 2 * HALO, HALF), F32),
            vmem((CHIP + 2 * HALO, HALF), F32),
            vmem((TALL, NL), F32),
            vmem((2, TALL, NL), F32),
            vmem((2, TALL, NL), BF16),
            vmem((2, SLABS - 1, BLOCK, BLOCK), BF16),
            vmem((2, BLOCK, SLABS * BLOCK), BF16),
            vmem((2, BLOCK, 512), F32),
            vmem((2, 3, BLOCK, 512), BF16),
            vmem((2, 3, BLOCK, 512), BF16),
            vmem((2, SIDE, SLABS, 16, BLOCK), BF16),
            vmem((SIDE, 16, NL), BF16),
            dma((COPIES,)), dma((COPIES,)), dma((8,)),
        ],
        compiler_params=pltpu.CompilerParams(collective_id=0, has_side_effects=True, vmem_limit_bytes=56203264),
    )(pltpu.with_memory_space_constraint(fine_model, pltpu.HBM), resample[0], lateral, shift, source[0], receiver[0])


def solution(mesh):
    in_specs = (
        P(("freq", "slab"), None),
        P("freq", "slab", None),
        P(),
        P("freq"),
        P("freq", "slab", None),
        P("freq", "slab", None),
    )
    out_specs = P(("freq", "slab"), None)
    return jax.shard_map(shards, mesh=mesh, in_specs=in_specs, out_specs=out_specs, check_vma=False)
```

```python
import functools

import jax
import jax.numpy as jnp
from jax import lax
from jax.experimental import pallas as pl
from jax.experimental.pallas import tpu as pltpu
from jax.sharding import PartitionSpec as P

SWEEPS = 8
HALO = 8
SIDE = 4
SLABS = 8
ROWS = 128
TALL = ROWS + 2 * HALO
CHIP = 2 * ROWS
NL = 2048
HALF = NL // 2
PATHS = (((1, 2, 0), 0, 384), ((2, 0, 1), 384, 384), ((0, 1, 2), 768, 256))
WIDE = NL // SLABS
BLOCK = 128
F32, BF16 = jnp.float32, jnp.bfloat16
MESH = pl.DeviceIdType.MESH


def turn(value, size):
    return lax.rem(value, size)


def ds(start, size, multiple=128):
    return pl.ds(pl.multiple_of(start, multiple), size)


class Links:
    def __init__(self, send, recv):
        self.send, self.recv, self.used, self.all = send, recv, 0, []

    def start(self, src, dst, to):
        copy = pltpu.make_async_remote_copy(
            src_ref=src, dst_ref=dst, send_sem=self.send.at[self.used], recv_sem=self.recv.at[self.used],
            device_id=to, device_id_type=MESH,
        )
        copy.start()
        self.used += 1
        self.all.append(copy)
        return copy

    def finish(self):
        for copy in self.all:
            copy.wait_send()


def migrate(fine, oper, lateral, shift, source, receiver, image,
            fa, fb, fc, lhs, edge, every, lat, src, rec, partial, invc, inv, field, narrow,
            turned, gathered, own, sent, came, sums, landed, send_sem, recv_sem, local_sem):
    freq, slab = lax.axis_index("freq"), lax.axis_index("slab")
    x, y, z, core = freq // SIDE, turn(freq, SIDE), slab // 2, turn(slab, 2)
    other = 1 - core

    def at(dx=0, dy=0, dz=0, dc=0):
        return {"freq": turn(x + dx, SIDE) * SIDE + turn(y + dy, SIDE),
                "slab": turn(z + dz, SIDE) * 2 + turn(core + dc, 2)}

    links = Links(send_sem, recv_sem)
    line = [{"freq": freq, "slab": turn(slab + d, SLABS)} for d in range(1, SLABS)]

    here = ds(slab * ROWS, ROWS)
    mine = ds(core * 16, 16, 16)
    local = {}
    for name, a, b in (
        (0, fine.at[:, ds(core * HALF, 384)], fa.at[x, y, z, mine]),
        (1, fine.at[:, ds(core * HALF + 384, 384)], fb.at[x, y, z, mine]),
        (2, fine.at[:, ds(core * HALF + 768, 256)], fc.at[x, y, z, mine]),
        ("lhs", oper, lhs.at[ds(core * ROWS, ROWS)]),
        ("every", oper, every.at[here]),
        ("src", source, src.at[HALO:HALO + ROWS]),
        ("lat", lateral, lat),
        ("rec", receiver, rec),
    ):
        local[name] = pltpu.make_async_copy(a, b, local_sem.at[len(local)])
        local[name].start()

    barrier = pltpu.get_barrier_semaphore()
    peers = line + [at(dx=d, dc=e) for d in (1, 2, 3) for e in (0, 1)] + [at(dy=d, dc=e) for d in (1, 2, 3) for e in (0, 1)]
    for peer in peers:
        pl.semaphore_signal(barrier, inc=1, device_id=peer, device_id_type=MESH)
    pl.semaphore_wait(barrier, len(peers))

    models = (fa, fb, fc)

    def along(axis, step, dc=0):
        return at(**{("dx", "dy", "dz")[axis]: step, "dc": dc})

    one, two, three, passed = {}, {}, {}, {}
    for path, (axes, first, size) in enumerate(PATHS):
        one[path] = [
            links.start(fine.at[:, ds(turn(core + e, 2) * HALF + first, size)], models[path].at[x, y, z, mine],
                        along(axes[0], d, e))
            for d in range(SIDE) for e in range(2) if d or e
        ]
    lined = []

    def part_of(block, quarter, quarters=1):
        return every.at[ds(block * ROWS + quarter * 32, 32 * quarters, 32)]

    def lend():
        part = part_of(slab, len(lined))
        lined.append((links.start(part, part, at(dz=1)), links.start(part, part, at(dz=3))))

    local["every"].wait()
    lend()
    order = (0, 3, 1, 2)

    def chunk(path, step, k, of_first=slice(None)):
        where = [x, y, z]
        axes = PATHS[path][0]
        where[axes[0]] = of_first
        where[axes[1]] = turn(where[axes[1]] + order[k], SIDE)
        where[axes[2]] = turn(where[axes[2]] + step, SIDE)
        return models[path].at[tuple(where)]

    def spread(path, k):
        part, axis = chunk(path, 0, k), PATHS[path][0][2]
        three[path, k] = (links.start(part, part, along(axis, 1)), links.start(part, part, along(axis, 3)))

    def forward(path, k):
        axis = PATHS[path][0][2]
        passed[path, k] = []
        for side, (came_from, to, of_first) in enumerate(((3, 1, slice(0, 2)), (1, 3, slice(2, 4)))):
            three[path, k][side].wait_recv()
            part = chunk(path, came_from, k, of_first)
            passed[path, k].append(links.start(part, part, along(axis, to)))

    every_path = range(len(PATHS))
    for path in every_path:
        local[path].wait()
        for copy in one[path]:
            copy.wait_recv()
        part, axis = chunk(path, 0, 0), PATHS[path][0][1]
        for k in (1, 2, 3):
            two[path, k] = links.start(part, part, along(axis, SIDE - order[k]))
            if k == 2:
                spread(path, 0)
    rows = links.start(oper, lhs.at[ds(core * ROWS, ROWS)], at(dc=1))
    early = []
    for e in range(2):
        to = {"freq": freq, "slab": turn(z + 3 - 2 * core, SIDE) * 2 + turn(core + e, 2)}
        early.append(links.start(oper.at[ds(core * (ROWS - 16), 16, 16)], edge.at[other], to))
    late = [
        links.start(source.at[ROWS - HALO:ROWS], src.at[0:HALO], line[0]),
        links.start(source.at[0:HALO], src.at[HALO + ROWS:TALL], line[SLABS - 2]),
    ]
    beside_core = links.start(every.at[here], every.at[here], at(dc=1))
    for k in (1, 2):
        for path in every_path:
            two[path, k].wait_recv()
            spread(path, k)
    for path in every_path:
        forward(path, 0)
    for path in every_path:
        two[path, 3].wait_recv()
        spread(path, 3)
    lend()
    for k in (1, 2, 3):
        for path in every_path:
            forward(path, k)
    lend()
    lend()

    for copy in early:
        copy.wait_recv()
    lhs[CHIP:CHIP + HALO] = edge[0, 16 - HALO:16]
    lhs[CHIP + HALO:CHIP + 2 * HALO] = edge[1, 0:HALO]
    local["lhs"].wait()
    rows.wait_recv()
    swapped = []

    def finish_coarse(path, coarse):
        axes, start, size = PATHS[path]
        columns = slice(start, start + size)
        part = 1.0 / (4.0 + shift[0] * coarse * coarse)
        invc[HALO:HALO + CHIP, columns] = part[:CHIP]
        invc[0:HALO, columns] = jnp.where(z > 0, part[CHIP:CHIP + HALO], 0.0)
        invc[HALO + CHIP:, columns] = jnp.where(z < SIDE - 1, part[CHIP + HALO:], 0.0)
        to = ds(core * HALF + start, size)
        swapped.append(links.start(invc.at[ds(other * ROWS, TALL), columns], inv.at[:, to], at(dc=1)))
        inv[:, to] = invc[ds(core * ROWS, TALL), columns]

    lefts, rights = {}, {}
    for k in range(SIDE):
        to = turn(x + (0, 3, 1, 2)[k], SIDE)
        lefts[0, k] = lefts[1, k] = lambda to=to: lhs[:, ds(to * 512, 512)]
        rights[0, k] = lambda to=to: fa[to].reshape(512, PATHS[0][2])
        rights[1, k] = lambda to=to: fb[to].reshape(512, PATHS[1][2])
        to = turn(y + (0, 3, 1, 2)[k], SIDE)
        lefts[2, k] = lambda to=to: jnp.concatenate([lhs[:, ds(m * 512 + to * BLOCK, BLOCK)] for m in range(SIDE)], axis=1)
        rights[2, k] = lambda to=to: fc[:, to].reshape(512, PATHS[2][2])

    for k in range(SIDE):
        for path, (axes, start, size) in enumerate(PATHS):
            if k == 3:
                if path == 0:
                    for step in range(SIDE):
                        for copy in passed[path, step]:
                            copy.wait_recv()
                else:
                    for copy in passed[path, k]:
                        copy.wait_recv()
            elif path:
                for copy in passed[path, k]:
                    copy.wait_recv()
            columns = slice(start, start + size)
            term = jnp.dot(lefts[path, k](), rights[path, k](), preferred_element_type=F32)
            if k == 0:
                partial[:, columns] = term
            elif k < 3:
                partial[:, columns] += term
            else:
                finish_coarse(path, partial[:, columns] + term)
    local["src"].wait()
    for copy in late + swapped:
        copy.wait_recv()
    for n in range(SIDE):
        columns = slice(n * 512, (n + 1) * 512)
        value = src[:, columns] * inv[:, columns]
        field[0, :, columns] = value
        narrow[0, :, columns] = value.astype(BF16)
    local["lat"].wait()
    local["rec"].wait()
    forwarded, crossed = [], []

    def pass_on(side, step, quarters):
        for quarter in range(SIDE):
            if quarter in quarters:
                lined[quarter][side].wait_recv()
                part = part_of(turn(z + 4 - step, SIDE) * 2 + core, quarter)
                forwarded.append(links.start(part, part, at(dz=step)))

    def cross(step):
        part = part_of(turn(z + step, SIDE) * 2 + core, 0, SIDE)
        crossed.append(links.start(part, part, at(dc=1)))

    pass_on(0, 1, (0,))
    pass_on(1, 3, (1,))
    for sweep in range(1, SWEEPS - 1):
        old, new = (sweep - 1) % 2, sweep % 2
        for n in range(SIDE):
            columns = slice(n * 512, (n + 1) * 512)
            side = jnp.dot(narrow[old], lat[:, columns], preferred_element_type=F32)
            before = field[old, :, columns]
            beside = pltpu.roll(before, 1, 0) + pltpu.roll(before, TALL - 1, 0)
            value = (src[:, columns] + 0.5 * beside + side) * inv[:, columns]
            field[new, :, columns] = value
            narrow[new, :, columns] = value.astype(BF16)
        if sweep == 3:
            pass_on(0, 1, (2,))
            pass_on(1, 3, (3,))
        if sweep == 4:
            for quarter in range(SIDE):
                lined[quarter][1 - quarter % 2].wait_recv()
            cross(3)
            cross(1)

    old = (SWEEPS - 2) % 2
    spans = {}
    for half in range(2):
        for pair in ((1, 2), (3, 4), (5, 6), (7, 0)):
            slices = [ds(turn(slab + d, SLABS) * WIDE + half * BLOCK, BLOCK) for d in pair]
            panel = jnp.concatenate([lat[:, columns] for columns in slices], axis=1)
            both = jnp.dot(narrow[old], panel, preferred_element_type=F32)
            for m, (d, columns) in enumerate(zip(pair, slices)):
                side = both[:, m * BLOCK:(m + 1) * BLOCK]
                before = field[old, :, columns]
                beside = pltpu.roll(before, 1, 0) + pltpu.roll(before, TALL - 1, 0)
                value = (src[:, columns] + 0.5 * beside + side) * inv[:, columns]
                part = (value[HALO:HALO + ROWS] * rec[:, columns]).T.astype(BF16)
                if d:
                    turned[half, d - 1] = part
                    spans[half, d] = links.start(turned.at[half, d - 1], gathered.at[half, :, here], line[d - 1])
                else:
                    gathered[half, :, here] = part
        if half == 0:
            for copy in forwarded:
                copy.wait_recv()
            cross(2)

    beside_core.wait_recv()
    for copy in crossed:
        copy.wait_recv()
    first, second = {}, []
    for half, me in ((0, x), (1, y)):
        for d in range(1, SLABS):
            spans[half, d].wait_recv()
        for d in (2, 1, 3, 0):
            to = turn(me + d, SIDE)
            if half == 0:
                panel = every[:, ds(to * 512, 512)]
            else:
                panel = jnp.concatenate([every[:, ds(m * 512 + to * BLOCK, BLOCK)] for m in range(SIDE)], axis=1)
            term = jnp.dot(gathered[half], panel, preferred_element_type=F32)
            if d:
                sent[half, d - 1] = term.astype(BF16)
                first[half, d] = links.start(sent.at[half, d - 1], came.at[half, d - 1], along(half, d))
            else:
                own[half] = term
    for half, it in ((0, y), (1, x)):
        total = own[half]
        for d in range(1, SIDE):
            first[half, d].wait_recv()
            total += came[half, d - 1].astype(F32)
        flat = total.T.astype(sums.dtype)
        for m in range(SIDE):
            for n in range(SLABS):
                sums[half, m, n] = flat[m * BLOCK + n * 16:m * BLOCK + (n + 1) * 16]
        to = ds(slab * WIDE + half * BLOCK, BLOCK)
        for d in (2, 1, 3, 0):
            for e in (4, 3, 5, 2, 6, 1, 7, 0):
                if d or e:
                    peer = along(1 - half, d)
                    peer["slab"] = turn(slab + e, SLABS)
                    second.append(links.start(sums.at[half, turn(it + d, SIDE), peer["slab"]], landed.at[d, :, to], peer))
        landed[0, :, to] = sums[half, it, slab]
    for copy in second:
        copy.wait_recv()
    image[...] = ((landed[0].astype(F32) + landed[1].astype(F32)) + (landed[2].astype(F32) + landed[3].astype(F32)))
    links.finish()


COPIES = 210


def shards(fine_model, resample, lateral, shift, source, receiver):
    anywhere = pl.BlockSpec(memory_space=pl.ANY)
    vmem, dma = pltpu.VMEM, pltpu.SemaphoreType.DMA
    return pl.pallas_call(
        migrate,
        name="migrate",
        out_shape=jax.ShapeDtypeStruct((16, NL), F32),
        in_specs=[anywhere, anywhere, anywhere, pl.BlockSpec(memory_space=pltpu.SMEM), anywhere, anywhere],
        out_specs=pl.BlockSpec(memory_space=pltpu.VMEM),
        scratch_shapes=[
            *(vmem((SIDE, SIDE, SIDE, 32, size), BF16) for _, _, size in PATHS),
            vmem((CHIP + 2 * HALO, NL), BF16),
            vmem((2, 16, NL), BF16),
            vmem((SLABS * ROWS, NL), BF16),
            vmem((NL, NL), BF16),
            vmem((TALL, NL), F32),
            vmem((ROWS, NL), F32),
            vmem((CHIP + 2 * HALO, HALF), F32),
            vmem((CHIP + 2 * HALO, HALF), F32),
            vmem((TALL, NL), F32),
            vmem((2, TALL, NL), F32),
            vmem((2, TALL, NL), BF16),
            vmem((2, SLABS - 1, BLOCK, BLOCK), BF16),
            vmem((2, BLOCK, SLABS * BLOCK), BF16),
            vmem((2, BLOCK, 512), F32),
            vmem((2, 3, BLOCK, 512), BF16),
            vmem((2, 3, BLOCK, 512), BF16),
            vmem((2, SIDE, SLABS, 16, BLOCK), BF16),
            vmem((SIDE, 16, NL), BF16),
            dma((COPIES,)), dma((COPIES,)), dma((8,)),
        ],
        compiler_params=pltpu.CompilerParams(collective_id=0, has_side_effects=True, vmem_limit_bytes=56203264),
    )(pltpu.with_memory_space_constraint(fine_model, pltpu.HBM), resample[0], lateral, shift, source[0], receiver[0])


def solution(mesh):
    in_specs = (
        P(("freq", "slab"), None),
        P("freq", "slab", None),
        P(),
        P("freq"),
        P("freq", "slab", None),
        P("freq", "slab", None),
    )
    out_specs = P(("freq", "slab"), None)
    return jax.shard_map(shards, mesh=mesh, in_specs=in_specs, out_specs=out_specs, check_vma=False)
```

```python
import functools

import jax
import jax.numpy as jnp
from jax import lax
from jax.experimental import pallas as pl
from jax.experimental.pallas import tpu as pltpu
from jax.sharding import PartitionSpec as P

SWEEPS = 8
HALO = 8
SIDE = 4
SLABS = 8
ROWS = 128
TALL = ROWS + 2 * HALO
CHIP = 2 * ROWS
NL = 2048
HALF = NL // 2
PATHS = (((1, 2, 0), 0, 384), ((2, 0, 1), 384, 384), ((0, 1, 2), 768, 256))
WIDE = NL // SLABS
BLOCK = 128
F32, BF16 = jnp.float32, jnp.bfloat16
MESH = pl.DeviceIdType.MESH


def turn(value, size):
    return lax.rem(value, size)


def ds(start, size, multiple=128):
    return pl.ds(pl.multiple_of(start, multiple), size)


class Links:
    def __init__(self, send, recv):
        self.send, self.recv, self.used, self.all = send, recv, 0, []

    def start(self, src, dst, to):
        copy = pltpu.make_async_remote_copy(
            src_ref=src, dst_ref=dst, send_sem=self.send.at[self.used], recv_sem=self.recv.at[self.used],
            device_id=to, device_id_type=MESH,
        )
        copy.start()
        self.used += 1
        self.all.append(copy)
        return copy

    def finish(self):
        for copy in self.all:
            copy.wait_send()


def migrate(fine, oper, lateral, shift, source, receiver, image,
            fa, fb, fc, lhs, edge, every, lat, src, rec, partial, invc, inv, field, narrow,
            turned, gathered, own, sent, came, sums, landed, send_sem, recv_sem, local_sem):
    freq, slab = lax.axis_index("freq"), lax.axis_index("slab")
    x, y, z, core = freq // SIDE, turn(freq, SIDE), slab // 2, turn(slab, 2)
    other = 1 - core

    def at(dx=0, dy=0, dz=0, dc=0):
        return {"freq": turn(x + dx, SIDE) * SIDE + turn(y + dy, SIDE),
                "slab": turn(z + dz, SIDE) * 2 + turn(core + dc, 2)}

    links = Links(send_sem, recv_sem)
    line = [{"freq": freq, "slab": turn(slab + d, SLABS)} for d in range(1, SLABS)]

    here = ds(slab * ROWS, ROWS)
    mine = ds(core * 16, 16, 16)
    local = {}
    for name, a, b in (
        (0, fine.at[:, ds(core * HALF, 384)], fa.at[x, y, z, mine]),
        (1, fine.at[:, ds(core * HALF + 384, 384)], fb.at[x, y, z, mine]),
        (2, fine.at[:, ds(core * HALF + 768, 256)], fc.at[x, y, z, mine]),
        ("lhs", oper, lhs.at[ds(core * ROWS, ROWS)]),
        ("every", oper, every.at[here]),
        ("src", source, src.at[HALO:HALO + ROWS]),
        ("lat", lateral, lat),
        ("rec", receiver, rec),
    ):
        local[name] = pltpu.make_async_copy(a, b, local_sem.at[len(local)])
        local[name].start()

    barrier = pltpu.get_barrier_semaphore()
    peers = line + [at(dx=d, dc=e) for d in (1, 2, 3) for e in (0, 1)] + [at(dy=d, dc=e) for d in (1, 2, 3) for e in (0, 1)]
    for peer in peers:
        pl.semaphore_signal(barrier, inc=1, device_id=peer, device_id_type=MESH)
    pl.semaphore_wait(barrier, len(peers))

    models = (fa, fb, fc)

    def along(axis, step, dc=0):
        return at(**{("dx", "dy", "dz")[axis]: step, "dc": dc})

    one, two, three, passed = {}, {}, {}, {}
    for path, (axes, first, size) in enumerate(PATHS):
        one[path] = [
            links.start(fine.at[:, ds(turn(core + e, 2) * HALF + first, size)], models[path].at[x, y, z, mine],
                        along(axes[0], d, e))
            for d in range(SIDE) for e in range(2) if d or e
        ]
    lined = []

    def part_of(block, quarter, quarters=1):
        return every.at[ds(block * ROWS + quarter * 32, 32 * quarters, 32)]

    def lend():
        part = part_of(slab, len(lined))
        lined.append((links.start(part, part, at(dz=1)), links.start(part, part, at(dz=3))))

    local["every"].wait()
    lend()
    order = (0, 3, 1, 2)

    def chunk(path, step, k, of_first=slice(None)):
        where = [x, y, z]
        axes = PATHS[path][0]
        where[axes[0]] = of_first
        where[axes[1]] = turn(where[axes[1]] + order[k], SIDE)
        where[axes[2]] = turn(where[axes[2]] + step, SIDE)
        return models[path].at[tuple(where)]

    def spread(path, k):
        part, axis = chunk(path, 0, k), PATHS[path][0][2]
        three[path, k] = (links.start(part, part, along(axis, 1)), links.start(part, part, along(axis, 3)))

    def forward(path, k):
        axis = PATHS[path][0][2]
        passed[path, k] = []
        for side, (came_from, to, of_first) in enumerate(((3, 1, slice(0, 2)), (1, 3, slice(2, 4)))):
            three[path, k][side].wait_recv()
            part = chunk(path, came_from, k, of_first)
            passed[path, k].append(links.start(part, part, along(axis, to)))

    every_path = range(len(PATHS))
    for path in every_path:
        local[path].wait()
        for copy in one[path]:
            copy.wait_recv()
        part, axis = chunk(path, 0, 0), PATHS[path][0][1]
        for k in (1, 2, 3):
            two[path, k] = links.start(part, part, along(axis, SIDE - order[k]))
            if k == 2:
                spread(path, 0)
    rows = links.start(oper, lhs.at[ds(core * ROWS, ROWS)], at(dc=1))
    early = []
    for e in range(2):
        to = {"freq": freq, "slab": turn(z + 3 - 2 * core, SIDE) * 2 + turn(core + e, 2)}
        early.append(links.start(oper.at[ds(core * (ROWS - 16), 16, 16)], edge.at[other], to))
    late = [
        links.start(source.at[ROWS - HALO:ROWS], src.at[0:HALO], line[0]),
        links.start(source.at[0:HALO], src.at[HALO + ROWS:TALL], line[SLABS - 2]),
    ]
    beside_core = links.start(every.at[here], every.at[here], at(dc=1))
    for k in (1, 2):
        for path in every_path:
            two[path, k].wait_recv()
            spread(path, k)
    for path in every_path:
        forward(path, 0)
    for path in every_path:
        two[path, 3].wait_recv()
        spread(path, 3)
    lend()
    for k in (1, 2, 3):
        for path in every_path:
            forward(path, k)
    lend()
    lend()

    for copy in early:
        copy.wait_recv()
    lhs[CHIP:CHIP + HALO] = edge[0, 16 - HALO:16]
    lhs[CHIP + HALO:CHIP + 2 * HALO] = edge[1, 0:HALO]
    local["lhs"].wait()
    rows.wait_recv()
    swapped = []

    def finish_coarse(path, coarse):
        axes, start, size = PATHS[path]
        columns = slice(start, start + size)
        part = 1.0 / (4.0 + shift[0] * coarse * coarse)
        invc[HALO:HALO + CHIP, columns] = part[:CHIP]
        invc[0:HALO, columns] = jnp.where(z > 0, part[CHIP:CHIP + HALO], 0.0)
        invc[HALO + CHIP:, columns] = jnp.where(z < SIDE - 1, part[CHIP + HALO:], 0.0)
        to = ds(core * HALF + start, size)
        swapped.append(links.start(invc.at[ds(other * ROWS, TALL), columns], inv.at[:, to], at(dc=1)))
        inv[:, to] = invc[ds(core * ROWS, TALL), columns]

    lefts, rights = {}, {}
    for k in range(SIDE):
        to = turn(x + (0, 3, 1, 2)[k], SIDE)
        lefts[0, k] = lefts[1, k] = lambda to=to: lhs[:, ds(to * 512, 512)]
        rights[0, k] = lambda to=to: fa[to].reshape(512, PATHS[0][2])
        rights[1, k] = lambda to=to: fb[to].reshape(512, PATHS[1][2])
        to = turn(y + (0, 3, 1, 2)[k], SIDE)
        lefts[2, k] = lambda to=to: jnp.concatenate([lhs[:, ds(m * 512 + to * BLOCK, BLOCK)] for m in range(SIDE)], axis=1)
        rights[2, k] = lambda to=to: fc[:, to].reshape(512, PATHS[2][2])

    for k in range(SIDE):
        for path, (axes, start, size) in enumerate(PATHS):
            if k == 3:
                if path == 0:
                    for step in range(SIDE):
                        for copy in passed[path, step]:
                            copy.wait_recv()
                else:
                    for copy in passed[path, k]:
                        copy.wait_recv()
            elif path:
                for copy in passed[path, k]:
                    copy.wait_recv()
            columns = slice(start, start + size)
            term = jnp.dot(lefts[path, k](), rights[path, k](), preferred_element_type=F32)
            if k == 0:
                partial[:, columns] = term
            elif k < 3:
                partial[:, columns] += term
            else:
                finish_coarse(path, partial[:, columns] + term)
    local["src"].wait()
    for copy in late:
        copy.wait_recv()

    def begin(half):
        for n in range(2):
            columns = ds(half * HALF + n * 512, 512)
            value = src[:, columns] * inv[:, columns]
            field[0, :, columns] = value
            narrow[0, :, columns] = value.astype(BF16)

    def side_of(half, columns):
        own_half = ds(half * HALF, HALF)
        return jnp.dot(narrow[0, :, own_half], lat[own_half, columns], preferred_element_type=F32)

    begin(core)
    local["lat"].wait()
    local["rec"].wait()
    for n in range(SIDE):
        columns = slice(n * 512, (n + 1) * 512)
        field[1, :, columns] = side_of(core, columns)
    for copy in swapped:
        copy.wait_recv()
    begin(other)
    forwarded, crossed = [], []

    def pass_on(side, step, quarters):
        for quarter in range(SIDE):
            if quarter in quarters:
                lined[quarter][side].wait_recv()
                part = part_of(turn(z + 4 - step, SIDE) * 2 + core, quarter)
                forwarded.append(links.start(part, part, at(dz=step)))

    def cross(step):
        part = part_of(turn(z + step, SIDE) * 2 + core, 0, SIDE)
        crossed.append(links.start(part, part, at(dc=1)))

    pass_on(0, 1, (0,))
    pass_on(1, 3, (1,))
    for sweep in range(1, SWEEPS - 1):
        old, new = (sweep - 1) % 2, sweep % 2
        for n in range(SIDE):
            columns = slice(n * 512, (n + 1) * 512)
            if sweep == 1:
                side = field[1, :, columns] + side_of(other, columns)
            else:
                side = jnp.dot(narrow[old], lat[:, columns], preferred_element_type=F32)
            before = field[old, :, columns]
            beside = pltpu.roll(before, 1, 0) + pltpu.roll(before, TALL - 1, 0)
            value = (src[:, columns] + 0.5 * beside + side) * inv[:, columns]
            field[new, :, columns] = value
            narrow[new, :, columns] = value.astype(BF16)
        if sweep == 3:
            pass_on(0, 1, (2,))
            pass_on(1, 3, (3,))
        if sweep == 4:
            for quarter in range(SIDE):
                lined[quarter][1 - quarter % 2].wait_recv()
            cross(3)
            cross(1)

    old = (SWEEPS - 2) % 2
    spans = {}
    for half in range(2):
        for pair in ((4, 3), (5, 2), (6, 1), (7, 0)):
            slices = [ds(turn(slab + d, SLABS) * WIDE + half * BLOCK, BLOCK) for d in pair]
            panel = jnp.concatenate([lat[:, columns] for columns in slices], axis=1)
            both = jnp.dot(narrow[old], panel, preferred_element_type=F32)
            for m, (d, columns) in enumerate(zip(pair, slices)):
                side = both[:, m * BLOCK:(m + 1) * BLOCK]
                before = field[old, :, columns]
                beside = pltpu.roll(before, 1, 0) + pltpu.roll(before, TALL - 1, 0)
                value = (src[:, columns] + 0.5 * beside + side) * inv[:, columns]
                part = (value[HALO:HALO + ROWS] * rec[:, columns]).T.astype(BF16)
                if d:
                    turned[half, d - 1] = part
                    spans[half, d] = links.start(turned.at[half, d - 1], gathered.at[half, :, here], line[d - 1])
                else:
                    gathered[half, :, here] = part
        if half == 0:
            for copy in forwarded:
                copy.wait_recv()
            cross(2)

    beside_core.wait_recv()
    for copy in crossed:
        copy.wait_recv()
    first, second = {}, []
    for half, me in ((0, x), (1, y)):
        for d in range(1, SLABS):
            spans[half, d].wait_recv()
        for d in (2, 1, 3, 0):
            to = turn(me + d, SIDE)
            if half == 0:
                panel = every[:, ds(to * 512, 512)]
            else:
                panel = jnp.concatenate([every[:, ds(m * 512 + to * BLOCK, BLOCK)] for m in range(SIDE)], axis=1)
            term = jnp.dot(gathered[half], panel, preferred_element_type=F32)
            if d:
                sent[half, d - 1] = term.astype(BF16)
                first[half, d] = links.start(sent.at[half, d - 1], came.at[half, d - 1], along(half, d))
            else:
                own[half] = term
    for half, it in ((0, y), (1, x)):
        total = own[half]
        for d in range(1, SIDE):
            first[half, d].wait_recv()
            total += came[half, d - 1].astype(F32)
        flat = total.T.astype(sums.dtype)
        for m in range(SIDE):
            for n in range(SLABS):
                sums[half, m, n] = flat[m * BLOCK + n * 16:m * BLOCK + (n + 1) * 16]
        to = ds(slab * WIDE + half * BLOCK, BLOCK)
        for d in (2, 1, 3, 0):
            for e in (4, 3, 5, 2, 6, 1, 7, 0):
                if d or e:
                    peer = along(1 - half, d)
                    peer["slab"] = turn(slab + e, SLABS)
                    second.append(links.start(sums.at[half, turn(it + d, SIDE), peer["slab"]], landed.at[d, :, to], peer))
        landed[0, :, to] = sums[half, it, slab]
    for copy in second:
        copy.wait_recv()
    image[...] = ((landed[0].astype(F32) + landed[1].astype(F32)) + (landed[2].astype(F32) + landed[3].astype(F32)))
    links.finish()


COPIES = 210


def shards(fine_model, resample, lateral, shift, source, receiver):
    anywhere = pl.BlockSpec(memory_space=pl.ANY)
    vmem, dma = pltpu.VMEM, pltpu.SemaphoreType.DMA
    return pl.pallas_call(
        migrate,
        name="migrate",
        out_shape=jax.ShapeDtypeStruct((16, NL), F32),
        in_specs=[anywhere, anywhere, anywhere, pl.BlockSpec(memory_space=pltpu.SMEM), anywhere, anywhere],
        out_specs=pl.BlockSpec(memory_space=pltpu.VMEM),
        scratch_shapes=[
            *(vmem((SIDE, SIDE, SIDE, 32, size), BF16) for _, _, size in PATHS),
            vmem((CHIP + 2 * HALO, NL), BF16),
            vmem((2, 16, NL), BF16),
            vmem((SLABS * ROWS, NL), BF16),
            vmem((NL, NL), BF16),
            vmem((TALL, NL), F32),
            vmem((ROWS, NL), F32),
            vmem((CHIP + 2 * HALO, HALF), F32),
            vmem((CHIP + 2 * HALO, HALF), F32),
            vmem((TALL, NL), F32),
            vmem((2, TALL, NL), F32),
            vmem((2, TALL, NL), BF16),
            vmem((2, SLABS - 1, BLOCK, BLOCK), BF16),
            vmem((2, BLOCK, SLABS * BLOCK), BF16),
            vmem((2, BLOCK, 512), F32),
            vmem((2, 3, BLOCK, 512), BF16),
            vmem((2, 3, BLOCK, 512), BF16),
            vmem((2, SIDE, SLABS, 16, BLOCK), BF16),
            vmem((SIDE, 16, NL), BF16),
            dma((COPIES,)), dma((COPIES,)), dma((8,)),
        ],
        compiler_params=pltpu.CompilerParams(collective_id=0, has_side_effects=True, vmem_limit_bytes=56203264),
    )(pltpu.with_memory_space_constraint(fine_model, pltpu.HBM), resample[0], lateral, shift, source[0], receiver[0])


def solution(mesh):
    in_specs = (
        P(("freq", "slab"), None),
        P("freq", "slab", None),
        P(),
        P("freq"),
        P("freq", "slab", None),
        P("freq", "slab", None),
    )
    out_specs = P(("freq", "slab"), None)
    return jax.shard_map(shards, mesh=mesh, in_specs=in_specs, out_specs=out_specs, check_vma=False)
```
